32 devices in a mesh: grp: 2 (over x), chol: 16 (over z, y, core).
Axes of the slice: x: 2, y: 2, z: 4, core: 2. Of those that a mesh axis runs over, the one named last changes fastest.
Arguments:
- chol_vectors: bfloat16 [2048, 32768], P(None, 'chol'), may hold values from -0.03125 to 0.03125
- mean_greens: bfloat16 [32768], P('chol'), may hold values from -6 to 6
- greens: bfloat16 [512, 32768], P(('grp', 'chol')), parts along dimension 0, may hold values from -6 to 6
- walker_order: int32 [512], P('grp'), parts along dimension 0, may hold values from 0 to 255, each once
- noise_field: float32 [512, 2048], P(('grp', 'chol')), parts along dimension 0, may hold values from -6 to 6
Outputs:
- shifted_field: float32 [512, 2048], P(('grp', 'chol')), parts along dimension 0
The draws below stay inside these ranges and needn't reach their ends.
There are 2 independent parts, one for each index of `grp`. The reference program is written for one: setup_inputs(seed, part) draws one part's arguments, and reference() takes and returns one part's arrays. A program takes and returns all parts, laid end to end along the dimension named above; an argument that names none is the same for every part. Nothing has to cross between parts.
Inputs may be any that keep to these rules, and one draw needn't show every extreme that they name: `walker_order`: each row of greens appears once.
All inputs are finite; a program needn't handle non-finite values.
Results may differ from the reference program's by a relative error of at most 0.0012.
Values may be sent and summed in bfloat16 or wider, within the bound.
A program may use at most 64 MiB of HBM per device.

```python
import jax
import jax.numpy as jnp

NCHOL = 2048
NP = 32768
W = 256


def strengthened(result, stream_key, source, target, shards_of, factor):
    def block_of(axis_at):
        return (jnp.arange(result.shape[axis_at]) // (result.shape[axis_at] // shards_of)).reshape((-1,) + (1,) * (result.ndim - 1 - axis_at))

    one_side = jax.random.permutation(stream_key, shards_of)[block_of(target)]
    other_side = (block_of(target) + shards_of // 2) % shards_of
    return jnp.where((block_of(source) == one_side) | (block_of(source) == other_side), factor * result, result)


def shard_levels(stream_key, dims, cuts, low, high):
    loudness = 1.0
    for dim, shards_of in cuts:
        draws = jax.random.uniform(jax.random.fold_in(jax.random.fold_in(stream_key, 6), dim), (shards_of,), jnp.float32, low / len(cuts), high / len(cuts))
        loudness = loudness * jnp.repeat(jnp.exp(draws), dims[dim] // shards_of).reshape((-1,) + (1,) * (len(dims) - 1 - dim))
    return loudness


def normal_values(key, shape, deviation, most, pieces=(), dtype=jnp.bfloat16):
    result = jax.random.normal(key, shape, jnp.float32) * deviation
    if len(pieces) > 0:
        result = shard_levels(key, shape, pieces, -0.22, 0.18) * result
    return jnp.clip(result, min=-most, max=most).astype(dtype)


def gaussian_with(own_key, shape, deviation, most, pieces, heavy, held_as=jnp.bfloat16):
    drawn = deviation * jax.random.normal(own_key, shape, jnp.float32)
    if pieces:
        drawn = drawn * shard_levels(own_key, shape, pieces, -0.22, 0.18)
    return jnp.clip(strengthened(drawn, jax.random.fold_in(own_key, 3), *heavy), -most, most).astype(held_as)


def setup_inputs(seed: int = 0, part: int = 0) -> dict:
    seeds = jax.random.split(jax.random.key(seed), 6)
    own_keys = jax.random.split(jax.random.fold_in(seeds[5], part), 6)
    chol_vectors = normal_values(seeds[0], (NCHOL, NP), NP ** -0.5, 0.03125, ((1, 16),))
    mean_greens = normal_values(seeds[1], (NP,), 1.0, 6.0, ((0, 16),))
    greens = gaussian_with(own_keys[2], (W, NP), 1.0, 6.0, ((0, 16),), (1, 0, 16, 2.0))
    walker_order = jax.random.permutation(own_keys[3], W).astype(jnp.int32)
    noise_field = normal_values(own_keys[4], (W, NCHOL), 1.0, 6.0, ((0, 16),), jnp.float32)
    return {"chol_vectors": chol_vectors, "mean_greens": mean_greens, "greens": greens, "walker_order": walker_order, "noise_field": noise_field}


def reference(chol_vectors, mean_greens, greens, walker_order, noise_field):
    picked = jnp.take(greens, walker_order.astype(jnp.int32), axis=0)
    raw_bias = jnp.dot(picked, chol_vectors.T, preferred_element_type=jnp.float32)
    mean_field = jnp.dot(chol_vectors, mean_greens, preferred_element_type=jnp.float32)
    shift = jnp.tanh(raw_bias) - mean_field[None, :]
    return noise_field - shift
```

```python
import functools

import jax
import jax.numpy as jnp
from jax import lax
from jax.experimental import pallas as pl
from jax.experimental.pallas import tpu as pltpu
from jax.sharding import PartitionSpec as P

CHUNKS = 4
LAST = 2
STEPS = 32000.0


def contract(left, right):
    return lax.dot_general(
        left, right, (((1,), (1,)), ((), ())), preferred_element_type=jnp.float32
    )


def encode(values):
    top = jnp.maximum(jnp.max(jnp.abs(values), axis=(0, 1), keepdims=True), 1e-30)
    return jnp.round(values * (STEPS / top)).astype(jnp.int32).astype(jnp.int16), top[0]


def decode(code, top):
    return code.astype(jnp.int32).astype(jnp.float32) * (top * (1.0 / STEPS))


def plain_per_device(chol_vectors, mean_greens, greens, walker_order, noise_field):
    pair_rows = lax.all_to_all(greens, "chol", split_axis=1, concat_axis=0, tiled=True)
    mean_part = jnp.dot(chol_vectors, mean_greens, preferred_element_type=jnp.float32)
    mean_field = lax.psum(mean_part, "chol")
    picked = jnp.take(pair_rows, walker_order, axis=0)
    raw_bias = lax.psum_scatter(
        contract(picked, chol_vectors), "chol", scatter_dimension=0, tiled=True
    )
    shift = jnp.tanh(raw_bias) - mean_field[None, :]
    return noise_field - shift


def order_key(mine, target, stage, r, dy, dc, p):
    to_middle = 0 < target[0] < 3
    cross = abs(r) >= 2 and not to_middle
    filler = (mine[0] == 0 and target[0] == 1) or (mine[0] == 1 and target == (2, mine[1]) and p == 0 and dc == 0)
    if not cross and not filler:
        stage = 99
    return (stage, p, -abs(r), -dy, dc, p)


def kernel(
    outer, inner,
    order_hbm, mean_hbm, noise_hbm, chol_hbm, greens_hbm, out_ref,
    order_ref, mean_ref, noise_ref, chol, rows_first, rows_last, chosen, part, core_in, y_out, y_code, y_top, y_in, y_top_in,
    z_out, z_code, z_top, z_in, z_top_in, mean_mine, mean_in,
    order_sem, mean_sem, noise_sem, chol_sem, own_sem, near_sem, a2a_send, a2a_recv,
    core_send, core_recv, y_send, y_recv, z_send, z_recv, mean_send, mean_recv,
):
    cores = 2
    n = outer * inner * cores
    walkers, pairs = greens_hbm.shape[0], chol.shape[1]
    nchol = chol.shape[0]
    width = nchol // CHUNKS
    rows = (rows_first, rows_last)
    starts = (0, rows_first.shape[2])
    me = lax.axis_index("chol")
    c = me % cores
    y = (me // cores) % inner
    z = me // (cores * inner)
    def device(zz, yy, cc):
        return (zz * inner + yy) * cores + cc

    def remote(src, dst, send, recv, target):
        return pltpu.make_async_remote_copy(
            src_ref=src, dst_ref=dst, send_sem=send, recv_sem=recv,
            device_id={"chol": target}, device_id_type=pl.DeviceIdType.MESH,
        )

    offsets = [
        (dz, dy, dc)
        for dz in range(outer) for dy in range(inner) for dc in range(cores)
        if (dz, dy, dc) != (0, 0, 0)
    ]

    def shifted(dz, dy, dc):
        return device((z + dz) % outer, (y + dy) % inner, (c + dc) % cores)

    core_peer = shifted(0, 0, 1)
    y_peer = shifted(0, 1, 0)

    def signal(sem, target):
        pl.semaphore_signal(
            sem, inc=1, device_id={"chol": target}, device_id_type=pl.DeviceIdType.MESH
        )

    barrier = pltpu.get_barrier_semaphore()
    chips = [(zz, yy) for zz in range(outer) for yy in range(inner)]

    @pl.when(c == 0)
    def _():
        signal(barrier, core_peer)

    for zz, yy in reversed(chips):
        @pl.when((zz >= z) & (yy >= y) & ((zz > z) | (yy > y)))
        def _():
            for cc in range(cores):
                signal(barrier, device(zz, yy, cc))

    chol_copy = pltpu.make_async_copy(chol_hbm, chol, chol_sem)
    order_copy = pltpu.make_async_copy(order_hbm, order_ref, order_sem)
    mean_copy = pltpu.make_async_copy(mean_hbm, mean_ref, mean_sem)
    noise_copy = pltpu.make_async_copy(noise_hbm, noise_ref, noise_sem)

    def span_of(owner, p):
        size = rows[p].shape[2]
        return pl.ds(pl.multiple_of(owner * pairs + starts[p], 128), size)

    own = [
        pltpu.make_async_copy(greens_hbm.at[:, span_of(me, p)], rows[p].at[me], own_sem.at[p])
        for p in range(2)
    ]
    a2a = []
    for p in range(2):
        a2a.append([])
        for k, offset in enumerate(offsets):
            target = shifted(*offset)
            a2a[p].append(remote(
                greens_hbm.at[:, span_of(target, p)], rows[p].at[me],
                a2a_send.at[p, k], a2a_recv.at[p, k], target,
            ))

    for copy in [order_copy, mean_copy, chol_copy, *own, noise_copy]:
        copy.start()
    below_here = cores * ((z + 1) * (y + 1) - 1) + c

    @pl.when(below_here > 0)
    def _():
        pl.semaphore_wait(barrier, below_here)

    here = z * inner + y

    @pl.when(c == cores - 1)
    def _():
        signal(near_sem.at[here], core_peer)
        for zz, yy in chips:
            @pl.when((zz <= z) & (yy <= y) & ((zz < z) | (yy < y)))
            def _():
                for cc in range(cores):
                    signal(near_sem.at[here], device(zz, yy, cc))

    for zv, yv in chips:
        far = 1 if zv < outer // 2 else -1
        above = [(zz, yy) for zz, yy in chips if zz >= zv and yy >= yv and (zz, yy) != (zv, yv)]
        below = {(zz, yy) for zz, yy in chips if zz <= zv and yy <= yv}
        waits, todo, left_over = [None, (zv, yv), *sorted(above, key=lambda a: (sum(a), a))], [], []
        known = below - {(zv, yv)}
        stage_of = {chip: 0 for chip in known}
        for stage, chip in enumerate(waits):
            if chip is not None:
                for zz, yy in chips:
                    if zz <= chip[0] and yy <= chip[1]:
                        stage_of.setdefault((zz, yy), stage)
        for p in range(2):
            for k, (dz, dy, dc) in enumerate(offsets):
                target = (zv + dz) % outer, (yv + dy) % inner
                r = (target[0] - zv) * far
                stage, *key = order_key((zv, yv), target, stage_of[target], r, dy, dc, p)
                todo.append((stage, key, p, k))
        todo.sort()

        @pl.when((z == zv) & (y == yv))
        def _():
            for stage, chip in enumerate(waits):
                if chip == (zv, yv):
                    @pl.when(c == 0)
                    def _():
                        pl.semaphore_wait(near_sem.at[zv * inner + yv], 1)
                elif chip is not None:
                    pl.semaphore_wait(near_sem.at[chip[0] * inner + chip[1]], 1)
                for when, _, p, k in todo:
                    if when == stage or (when > stage and stage == len(waits) - 1):
                        a2a[p][k].start()

    order_copy.wait()
    source = lax.broadcasted_iota(jnp.int32, (n * walkers, n * walkers), 0)
    chosen[...] = jnp.where(source == order_ref[...], 1.0, 0.0).T.astype(jnp.bfloat16)

    mean_copy.wait()
    chol_copy.wait()
    mean_rows = jnp.broadcast_to(mean_ref[...].astype(jnp.float32).reshape(1, pairs), (16, pairs)).astype(jnp.bfloat16)
    for q in range(CHUNKS):
        span = pl.ds(q * width, width)
        mean_mine[0, :, span] = contract(mean_rows, chol[span, :])[0:1, :]

    def mean_hop(at, stage, target):
        return remote(
            mean_mine.at[at], mean_in.at[stage], mean_send.at[stage], mean_recv.at[stage], target
        )

    core_hop = mean_hop(0, 0, core_peer)
    y_hop = mean_hop(1, 1, y_peer)
    z_hops = [mean_hop(2, 1 + dz, shifted(dz, 0, 0)) for dz in range(1, outer)]
    core_hop.start()
    core_hop.wait()
    mean_mine[1] = mean_mine[0] + mean_in[0]
    y_hop.start()

    def pick(p):
        own[p].wait()
        for copy in a2a[p]:
            copy.wait_recv()
        size = rows[p].shape[2]
        return jnp.dot(
            chosen[...], rows[p][...].reshape(n * walkers, size), preferred_element_type=jnp.float32
        ).astype(jnp.bfloat16)

    def add(p, picked, q):
        size = rows[p].shape[2]
        bias = contract(picked, chol[pl.ds(q * width, width), pl.ds(starts[p], size)])
        bias = bias.reshape(outer * inner, cores, walkers, width)
        for cc in range(cores):
            part[q, cc] = bias[:, cc] if p == 0 else part[q, cc] + bias[:, cc]

    picked = pick(0)
    for q in range(CHUNKS):
        add(0, picked, q)
    y_hop.wait()
    mean_mine[2] = mean_mine[1] + mean_in[1]
    for hop in z_hops:
        hop.start()
    picked = pick(1)

    def core_copy(q):
        return remote(
            part.at[q, 1 - c], core_in.at[q], core_send.at[q], core_recv.at[q], core_peer
        )

    half = outer // 2

    def y_copies(q, h):
        return (
            remote(y_code.at[q, h], y_in.at[q, h], y_send.at[q, h, 0], y_recv.at[q, h, 0], y_peer),
            remote(y_top.at[q, h], y_top_in.at[q, h], y_send.at[q, h, 1], y_recv.at[q, h, 1], y_peer),
        )

    def z_copies(q, h, at, slot, zz, target):
        return (
            remote(z_code.at[q, h, at], z_in.at[q, slot], z_send.at[q, zz, 0], z_recv.at[q, slot, 0], target),
            remote(z_top.at[q, h], z_top_in.at[q, slot], z_send.at[q, zz, 1], z_recv.at[q, slot, 1], target),
        )

    def send_y(q, h):
        y_code[q, h], y_top[q, h] = encode(y_out[q, 1 - y, half * h:half * (h + 1)])
        for copy in y_copies(q, h):
            copy.start()

    def sum_cores(q):
        core_copy(q).wait()
        total = (part[q, c] + core_in[q]).reshape(outer, inner, walkers, width)
        for yy in range(inner):
            y_out[q, yy] = total[:, yy]
        send_y(q, 0)

    def sum_inner(q, h):
        for copy in y_copies(q, h):
            copy.wait()
        total = y_out[q, y, half * h:half * (h + 1)] + decode(y_in[q, h], y_top_in[q, h])
        z_out[q, half * h:half * (h + 1)] = total
        z_code[q, h], z_top[q, h] = encode(total)
        for at in range(half):
            zz = half * h + at

            @pl.when(z != zz)
            def _():
                for copy in z_copies(q, h, at, z, zz, device(zz, y, c)):
                    copy.start()

    def finish(q):
        span = pl.ds(q * width, width)
        raw = z_out[q, z]
        for dz in range(1, outer):
            zz = (z + dz) % outer
            for copy in z_copies(q, 0, 0, zz, zz, device(zz, y, c)):
                copy.wait_recv()
            raw = raw + decode(z_in[q, zz], z_top_in[q, zz])
        out_ref[:, span] = noise_ref[:, span] - (jnp.tanh(raw) - mean_mine[3, :, span])

    for step in range(CHUNKS + 1):
        if step < CHUNKS:
            add(1, picked, step)
            core_copy(step).start()
        if step >= 1:
            sum_cores(step - 1)
    for q in range(CHUNKS):
        send_y(q, 1)
    for h in range(2):
        for q in range(CHUNKS):
            sum_inner(q, h)
    noise_copy.wait()
    for hop in z_hops:
        hop.wait()
    mean = mean_mine[2]
    for dz in range(1, outer):
        mean = mean + mean_in[1 + dz]
    mean_mine[3] = mean
    for q in range(CHUNKS):
        finish(q)
    for q in range(CHUNKS):
        for dz in range(1, outer):
            zz = (z + dz) % outer
            for copy in z_copies(q, 0, 0, zz, zz, device(zz, y, c)):
                copy.wait_send()
    for p in range(2):
        for copy in a2a[p]:
            copy.wait_send()


def fused_per_device(outer, inner, chol_vectors, mean_greens, greens, walker_order, noise_field):
    nchol, pairs = chol_vectors.shape
    walkers = greens.shape[0]
    n = outer * inner * 2
    width = nchol // CHUNKS
    last = pairs // LAST
    halves = (CHUNKS, 2, outer // 2, walkers, width)
    vmem = pl.BlockSpec(memory_space=pltpu.VMEM)
    hbm = pl.BlockSpec(memory_space=pltpu.HBM)
    dma = pltpu.SemaphoreType.DMA
    f32, i16 = jnp.float32, jnp.int16
    return pl.pallas_call(
        functools.partial(kernel, outer, inner),
        out_shape=pltpu.VMEM(noise_field.shape, f32),
        in_specs=[hbm] * 5,
        out_specs=vmem,
        scratch_shapes=[
            pltpu.VMEM((1, n * walkers), jnp.int32),
            pltpu.VMEM((pairs,), jnp.bfloat16),
            pltpu.VMEM(noise_field.shape, f32),
            pltpu.VMEM((nchol, pairs), jnp.bfloat16),
            pltpu.VMEM((n, walkers, pairs - last), jnp.bfloat16),
            pltpu.VMEM((n, walkers, last), jnp.bfloat16),
            pltpu.VMEM((n * walkers, n * walkers), jnp.bfloat16),
            pltpu.VMEM((CHUNKS, 2, outer * inner, walkers, width), f32),
            pltpu.VMEM((CHUNKS, outer * inner, walkers, width), f32),
            pltpu.VMEM((CHUNKS, inner, outer, walkers, width), f32),
            *[pltpu.VMEM(halves, i16), pltpu.VMEM((CHUNKS, 2, 1, width), f32)] * 2,
            pltpu.VMEM((CHUNKS, outer, walkers, width), f32),
            pltpu.VMEM(halves, i16), pltpu.VMEM((CHUNKS, 2, 1, width), f32),
            pltpu.VMEM((CHUNKS, outer, walkers, width), i16), pltpu.VMEM((CHUNKS, outer, 1, width), f32),
            pltpu.VMEM((4, 1, nchol), f32),
            pltpu.VMEM((1 + outer, 1, nchol), f32),
            dma, dma, dma, dma, dma((2,)), pltpu.SemaphoreType.REGULAR((outer * inner,)),
            dma((2, n - 1)), dma((2, n - 1)),
            dma((CHUNKS,)), dma((CHUNKS,)), dma((CHUNKS, 2, 2)), dma((CHUNKS, 2, 2)),
            dma((CHUNKS, outer, 2)), dma((CHUNKS, outer, 2)),
            dma((1 + outer,)), dma((1 + outer,)),
        ],
        compiler_params=pltpu.CompilerParams(
            collective_id=0, has_side_effects=True, vmem_limit_bytes=60 * 1024 * 1024
        ),
    )(walker_order[None, :], mean_greens, noise_field, chol_vectors, greens)


def solution(mesh):
    placed = (
        P(None, "chol"),
        P("chol"),
        P(("grp", "chol"), None),
        P("grp"),
        P(("grp", "chol"), None),
    )
    chips = mesh.shape["chol"] // 2
    inner = 1
    while (2 * inner) ** 2 <= chips:
        inner *= 2
    outer = chips // inner
    body = functools.partial(fused_per_device, outer, inner) if (outer, inner) == (4, 2) else plain_per_device
    return jax.shard_map(
        body, mesh=mesh, in_specs=placed, out_specs=P(("grp", "chol"), None), check_vma=False
    )
```

```python
import functools

import jax
import jax.numpy as jnp
from jax import lax
from jax.experimental import pallas as pl
from jax.experimental.pallas import tpu as pltpu
from jax.sharding import PartitionSpec as P

CHUNKS = 4
LAST = 2
STEPS = 32000.0


def contract(left, right):
    return lax.dot_general(
        left, right, (((1,), (1,)), ((), ())), preferred_element_type=jnp.float32
    )


def encode(values):
    top = jnp.maximum(jnp.max(jnp.abs(values), axis=(0, 1), keepdims=True), 1e-30)
    return jnp.round(values * (STEPS / top)).astype(jnp.int32).astype(jnp.int16), top[0]


def decode(code, top):
    return code.astype(jnp.int32).astype(jnp.float32) * (top * (1.0 / STEPS))


def plain_per_device(chol_vectors, mean_greens, greens, walker_order, noise_field):
    pair_rows = lax.all_to_all(greens, "chol", split_axis=1, concat_axis=0, tiled=True)
    mean_part = jnp.dot(chol_vectors, mean_greens, preferred_element_type=jnp.float32)
    mean_field = lax.psum(mean_part, "chol")
    picked = jnp.take(pair_rows, walker_order, axis=0)
    raw_bias = lax.psum_scatter(
        contract(picked, chol_vectors), "chol", scatter_dimension=0, tiled=True
    )
    shift = jnp.tanh(raw_bias) - mean_field[None, :]
    return noise_field - shift


def order_key(mine, target, stage, r, dy, dc, p):
    to_middle = 0 < target[0] < 3
    cross = abs(r) >= 2 and not to_middle
    filler = (mine[0] == 0 and target[0] == 1) or (mine[0] == 1 and target == (2, mine[1]) and p == 0)
    if not cross and not filler:
        stage = 99
    return (stage, p, -abs(r), -dy, dc)


def kernel(
    outer, inner,
    order_hbm, mean_hbm, noise_hbm, chol_hbm, greens_hbm, out_ref,
    order_ref, mean_ref, noise_ref, chol, rows_first, rows_last, chosen, part, core_in, y_code, y_top, y_in, y_top_in,
    z_out, z_code, z_top, z_in, z_top_in, mean_mine, mean_in,
    order_sem, mean_sem, noise_sem, chol_sem, own_sem, near_sem, a2a_send, a2a_recv,
    core_send, core_recv, y_send, y_recv, z_send, z_recv, mean_send, mean_recv,
):
    cores = 2
    n = outer * inner * cores
    walkers, pairs = greens_hbm.shape[0], chol.shape[1]
    nchol = chol.shape[0]
    width = nchol // CHUNKS
    rows = (rows_first, rows_last)
    starts = (0, rows_first.shape[2])
    me = lax.axis_index("chol")
    c = me % cores
    y = (me // cores) % inner
    z = me // (cores * inner)
    def device(zz, yy, cc):
        return (zz * inner + yy) * cores + cc

    def remote(src, dst, send, recv, target):
        return pltpu.make_async_remote_copy(
            src_ref=src, dst_ref=dst, send_sem=send, recv_sem=recv,
            device_id={"chol": target}, device_id_type=pl.DeviceIdType.MESH,
        )

    offsets = [
        (dz, dy, dc)
        for dz in range(outer) for dy in range(inner) for dc in range(cores)
        if (dz, dy, dc) != (0, 0, 0)
    ]

    def shifted(dz, dy, dc):
        return device((z + dz) % outer, (y + dy) % inner, (c + dc) % cores)

    core_peer = shifted(0, 0, 1)
    y_peer = shifted(0, 1, 0)

    def signal(sem, target):
        pl.semaphore_signal(
            sem, inc=1, device_id={"chol": target}, device_id_type=pl.DeviceIdType.MESH
        )

    barrier = pltpu.get_barrier_semaphore()
    chips = [(zz, yy) for zz in range(outer) for yy in range(inner)]

    @pl.when(c == 0)
    def _():
        signal(barrier, core_peer)

    for zz, yy in reversed(chips):
        @pl.when((zz >= z) & (yy >= y) & ((zz > z) | (yy > y)))
        def _():
            for cc in range(cores):
                signal(barrier, device(zz, yy, cc))

    chol_copy = pltpu.make_async_copy(chol_hbm, chol, chol_sem)
    order_copy = pltpu.make_async_copy(order_hbm, order_ref, order_sem)
    mean_copy = pltpu.make_async_copy(mean_hbm, mean_ref, mean_sem)
    noise_copy = pltpu.make_async_copy(noise_hbm, noise_ref, noise_sem)

    def span_of(owner, p):
        size = rows[p].shape[2]
        return pl.ds(pl.multiple_of(owner * pairs + starts[p], 128), size)

    own = [
        pltpu.make_async_copy(greens_hbm.at[:, span_of(me, p)], rows[p].at[me], own_sem.at[p])
        for p in range(2)
    ]
    a2a = []
    for p in range(2):
        a2a.append([])
        for k, offset in enumerate(offsets):
            target = shifted(*offset)
            a2a[p].append(remote(
                greens_hbm.at[:, span_of(target, p)], rows[p].at[me],
                a2a_send.at[p, k], a2a_recv.at[p, k], target,
            ))

    for copy in [order_copy, mean_copy, chol_copy, *own, noise_copy]:
        copy.start()
    below_here = cores * ((z + 1) * (y + 1) - 1) + c

    @pl.when(below_here > 0)
    def _():
        pl.semaphore_wait(barrier, below_here)

    here = z * inner + y

    @pl.when(c == cores - 1)
    def _():
        signal(near_sem.at[here], core_peer)
        for zz, yy in chips:
            @pl.when((zz <= z) & (yy <= y) & ((zz < z) | (yy < y)))
            def _():
                for cc in range(cores):
                    signal(near_sem.at[here], device(zz, yy, cc))

    for zv, yv in chips:
        far = 1 if zv < outer // 2 else -1
        above = [(zz, yy) for zz, yy in chips if zz >= zv and yy >= yv and (zz, yy) != (zv, yv)]
        below = {(zz, yy) for zz, yy in chips if zz <= zv and yy <= yv}
        waits, todo, left_over = [None, (zv, yv), *sorted(above, key=lambda a: (sum(a), a))], [], []
        known = below - {(zv, yv)}
        stage_of = {chip: 0 for chip in known}
        for stage, chip in enumerate(waits):
            if chip is not None:
                for zz, yy in chips:
                    if zz <= chip[0] and yy <= chip[1]:
                        stage_of.setdefault((zz, yy), stage)
        for p in range(2):
            for k, (dz, dy, dc) in enumerate(offsets):
                target = (zv + dz) % outer, (yv + dy) % inner
                r = (target[0] - zv) * far
                stage, *key = order_key((zv, yv), target, stage_of[target], r, dy, dc, p)
                todo.append((stage, key, p, k))
        todo.sort()

        @pl.when((z == zv) & (y == yv))
        def _():
            for stage, chip in enumerate(waits):
                if chip == (zv, yv):
                    @pl.when(c == 0)
                    def _():
                        pl.semaphore_wait(near_sem.at[zv * inner + yv], 1)
                elif chip is not None:
                    pl.semaphore_wait(near_sem.at[chip[0] * inner + chip[1]], 1)
                for when, _, p, k in todo:
                    if when == stage or (when > stage and stage == len(waits) - 1):
                        a2a[p][k].start()

    order_copy.wait()
    source = lax.broadcasted_iota(jnp.int32, (n * walkers, n * walkers), 0)
    chosen[...] = jnp.where(source == order_ref[...], 1.0, 0.0).T.astype(jnp.bfloat16)

    mean_copy.wait()
    chol_copy.wait()
    mean_rows = jnp.broadcast_to(mean_ref[...].astype(jnp.float32).reshape(1, pairs), (16, pairs)).astype(jnp.bfloat16)
    for q in range(CHUNKS):
        span = pl.ds(q * width, width)
        mean_mine[0, :, span] = contract(mean_rows, chol[span, :])[0:1, :]

    def mean_hop(at, stage, target):
        return remote(
            mean_mine.at[at], mean_in.at[stage], mean_send.at[stage], mean_recv.at[stage], target
        )

    core_hop = mean_hop(0, 0, core_peer)
    y_hop = mean_hop(1, 1, y_peer)
    z_hops = [mean_hop(2, 1 + dz, shifted(dz, 0, 0)) for dz in range(1, outer)]
    core_hop.start()
    core_hop.wait()
    mean_mine[1] = mean_mine[0] + mean_in[0]
    y_hop.start()

    def pick(p):
        own[p].wait()
        for copy in a2a[p]:
            copy.wait_recv()
        size = rows[p].shape[2]
        return jnp.dot(
            chosen[...], rows[p][...].reshape(n * walkers, size), preferred_element_type=jnp.float32
        ).astype(jnp.bfloat16)

    def add(p, picked, q):
        size = rows[p].shape[2]
        bias = contract(picked, chol[pl.ds(q * width, width), pl.ds(starts[p], size)])
        bias = bias.reshape(outer, inner, cores, walkers, width)
        for cc in range(cores):
            part[q, cc] = bias[:, :, cc] if p == 0 else part[q, cc] + bias[:, :, cc]

    picked = pick(0)
    for q in range(CHUNKS):
        add(0, picked, q)
    y_hop.wait()
    mean_mine[2] = mean_mine[1] + mean_in[1]
    for hop in z_hops:
        hop.start()
    picked = pick(1)

    def core_copy(q):
        return remote(
            part.at[q, 1 - c], core_in.at[q], core_send.at[q], core_recv.at[q], core_peer
        )

    half = outer // 2

    def y_copies(q, h):
        return (
            remote(y_code.at[q, h], y_in.at[q, h], y_send.at[q, h, 0], y_recv.at[q, h, 0], y_peer),
            remote(y_top.at[q, h], y_top_in.at[q, h], y_send.at[q, h, 1], y_recv.at[q, h, 1], y_peer),
        )

    def z_copies(q, h, at, slot, zz, target):
        return (
            remote(z_code.at[q, h, at], z_in.at[q, slot], z_send.at[q, zz, 0], z_recv.at[q, slot, 0], target),
            remote(z_top.at[q, h], z_top_in.at[q, slot], z_send.at[q, zz, 1], z_recv.at[q, slot, 1], target),
        )

    def both_cores(q, h, yy):
        z_part = pl.ds(half * h, half)
        return part[q, c, z_part, yy] + core_in[q, z_part, yy]

    def send_y(q, h):
        y_code[q, h], y_top[q, h] = encode(both_cores(q, h, 1 - y))
        for copy in y_copies(q, h):
            copy.start()

    def sum_cores(q):
        core_copy(q).wait()
        send_y(q, 0)

    def sum_inner(q, h):
        for copy in y_copies(q, h):
            copy.wait()
        total = both_cores(q, h, y) + decode(y_in[q, h], y_top_in[q, h])
        z_out[q, half * h:half * (h + 1)] = total
        z_code[q, h], z_top[q, h] = encode(total)
        for at in range(half):
            zz = half * h + at

            @pl.when(z != zz)
            def _():
                for copy in z_copies(q, h, at, z, zz, device(zz, y, c)):
                    copy.start()

    def finish(q):
        span = pl.ds(q * width, width)
        raw = z_out[q, z]
        for dz in range(1, outer):
            zz = (z + dz) % outer
            for copy in z_copies(q, 0, 0, zz, zz, device(zz, y, c)):
                copy.wait_recv()
            raw = raw + decode(z_in[q, zz], z_top_in[q, zz])
        out_ref[:, span] = noise_ref[:, span] - (jnp.tanh(raw) - mean_mine[3, :, span])

    for step in range(CHUNKS + 2):
        if step < CHUNKS:
            add(1, picked, step)
            core_copy(step).start()
        if step >= 2:
            sum_cores(step - 2)
    for q in range(CHUNKS):
        send_y(q, 1)
    for h in range(2):
        for q in range(CHUNKS):
            sum_inner(q, h)
    noise_copy.wait()
    for hop in z_hops:
        hop.wait()
    mean = mean_mine[2]
    for dz in range(1, outer):
        mean = mean + mean_in[1 + dz]
    mean_mine[3] = mean
    for q in range(CHUNKS):
        finish(q)
    for q in range(CHUNKS):
        for dz in range(1, outer):
            zz = (z + dz) % outer
            for copy in z_copies(q, 0, 0, zz, zz, device(zz, y, c)):
                copy.wait_send()
    for p in range(2):
        for copy in a2a[p]:
            copy.wait_send()


def fused_per_device(outer, inner, chol_vectors, mean_greens, greens, walker_order, noise_field):
    nchol, pairs = chol_vectors.shape
    walkers = greens.shape[0]
    n = outer * inner * 2
    width = nchol // CHUNKS
    last = pairs // LAST
    halves = (CHUNKS, 2, outer // 2, walkers, width)
    vmem = pl.BlockSpec(memory_space=pltpu.VMEM)
    hbm = pl.BlockSpec(memory_space=pltpu.HBM)
    dma = pltpu.SemaphoreType.DMA
    f32, i16 = jnp.float32, jnp.int16
    return pl.pallas_call(
        functools.partial(kernel, outer, inner),
        out_shape=pltpu.VMEM(noise_field.shape, f32),
        in_specs=[hbm] * 5,
        out_specs=vmem,
        scratch_shapes=[
            pltpu.VMEM((1, n * walkers), jnp.int32),
            pltpu.VMEM((pairs,), jnp.bfloat16),
            pltpu.VMEM(noise_field.shape, f32),
            pltpu.VMEM((nchol, pairs), jnp.bfloat16),
            pltpu.VMEM((n, walkers, pairs - last), jnp.bfloat16),
            pltpu.VMEM((n, walkers, last), jnp.bfloat16),
            pltpu.VMEM((n * walkers, n * walkers), jnp.bfloat16),
            pltpu.VMEM((CHUNKS, 2, outer, inner, walkers, width), f32),
            pltpu.VMEM((CHUNKS, outer, inner, walkers, width), f32),
            *[pltpu.VMEM(halves, i16), pltpu.VMEM((CHUNKS, 2, 1, width), f32)] * 2,
            pltpu.VMEM((CHUNKS, outer, walkers, width), f32),
            pltpu.VMEM(halves, i16), pltpu.VMEM((CHUNKS, 2, 1, width), f32),
            pltpu.VMEM((CHUNKS, outer, walkers, width), i16), pltpu.VMEM((CHUNKS, outer, 1, width), f32),
            pltpu.VMEM((4, 1, nchol), f32),
            pltpu.VMEM((1 + outer, 1, nchol), f32),
            dma, dma, dma, dma, dma((2,)), pltpu.SemaphoreType.REGULAR((outer * inner,)),
            dma((2, n - 1)), dma((2, n - 1)),
            dma((CHUNKS,)), dma((CHUNKS,)), dma((CHUNKS, 2, 2)), dma((CHUNKS, 2, 2)),
            dma((CHUNKS, outer, 2)), dma((CHUNKS, outer, 2)),
            dma((1 + outer,)), dma((1 + outer,)),
        ],
        compiler_params=pltpu.CompilerParams(
            collective_id=0, has_side_effects=True, vmem_limit_bytes=60 * 1024 * 1024
        ),
    )(walker_order[None, :], mean_greens, noise_field, chol_vectors, greens)


def solution(mesh):
    placed = (
        P(None, "chol"),
        P("chol"),
        P(("grp", "chol"), None),
        P("grp"),
        P(("grp", "chol"), None),
    )
    chips = mesh.shape["chol"] // 2
    inner = 1
    while (2 * inner) ** 2 <= chips:
        inner *= 2
    outer = chips // inner
    body = functools.partial(fused_per_device, outer, inner) if (outer, inner) == (4, 2) else plain_per_device
    return jax.shard_map(
        body, mesh=mesh, in_specs=placed, out_specs=P(("grp", "chol"), None), check_vma=False
    )
```

```python
import functools

import jax
import jax.numpy as jnp
from jax import lax
from jax.experimental import pallas as pl
from jax.experimental.pallas import tpu as pltpu
from jax.sharding import PartitionSpec as P

CHUNKS = 4
LAST = 2
STEPS = 32000.0


def contract(left, right):
    return lax.dot_general(
        left, right, (((1,), (1,)), ((), ())), preferred_element_type=jnp.float32
    )


def encode(values):
    top = jnp.maximum(jnp.max(jnp.abs(values), axis=(0, 1), keepdims=True), 1e-30)
    return jnp.round(values * (STEPS / top)).astype(jnp.int32).astype(jnp.int16), top[0]


def decode(code, top):
    return code.astype(jnp.int32).astype(jnp.float32) * (top * (1.0 / STEPS))


def plain_per_device(chol_vectors, mean_greens, greens, walker_order, noise_field):
    pair_rows = lax.all_to_all(greens, "chol", split_axis=1, concat_axis=0, tiled=True)
    mean_part = jnp.dot(chol_vectors, mean_greens, preferred_element_type=jnp.float32)
    mean_field = lax.psum(mean_part, "chol")
    picked = jnp.take(pair_rows, walker_order, axis=0)
    raw_bias = lax.psum_scatter(
        contract(picked, chol_vectors), "chol", scatter_dimension=0, tiled=True
    )
    shift = jnp.tanh(raw_bias) - mean_field[None, :]
    return noise_field - shift


def order_key(mine, target, stage, r, dy, dc, p):
    to_middle = 0 < target[0] < 3
    cross = abs(r) >= 2 and not to_middle
    filler = (mine[0] == 0 and target[0] == 1) or (mine[0] == 1 and target == (2, mine[1]) and p == 0)
    if not cross and not filler:
        stage = 99
    return (stage, p, -abs(r), -dy, dc)


def kernel(
    outer, inner,
    order_hbm, mean_hbm, noise_hbm, chol_hbm, greens_hbm, out_ref,
    order_ref, mean_ref, noise_ref, chol, rows_first, rows_last, chosen, part, core_in, y_code, y_top, y_in, y_top_in,
    z_out, z_code, z_top, z_in, z_top_in, mean_mine, mean_in,
    order_sem, mean_sem, noise_sem, chol_sem, own_sem, near_sem, a2a_send, a2a_recv,
    core_send, core_recv, y_send, y_recv, z_send, z_recv, mean_send, mean_recv,
):
    cores = 2
    n = outer * inner * cores
    walkers, pairs = greens_hbm.shape[0], chol.shape[1]
    nchol = chol.shape[0]
    width = nchol // CHUNKS
    rows = (rows_first, rows_last)
    starts = (0, rows_first.shape[2])
    me = lax.axis_index("chol")
    c = me % cores
    y = (me // cores) % inner
    z = me // (cores * inner)
    def device(zz, yy, cc):
        return (zz * inner + yy) * cores + cc

    def remote(src, dst, send, recv, target):
        return pltpu.make_async_remote_copy(
            src_ref=src, dst_ref=dst, send_sem=send, recv_sem=recv,
            device_id={"chol": target}, device_id_type=pl.DeviceIdType.MESH,
        )

    offsets = [
        (dz, dy, dc)
        for dz in range(outer) for dy in range(inner) for dc in range(cores)
        if (dz, dy, dc) != (0, 0, 0)
    ]

    def shifted(dz, dy, dc):
        return device((z + dz) % outer, (y + dy) % inner, (c + dc) % cores)

    core_peer = shifted(0, 0, 1)
    y_peer = shifted(0, 1, 0)

    def signal(sem, target):
        pl.semaphore_signal(
            sem, inc=1, device_id={"chol": target}, device_id_type=pl.DeviceIdType.MESH
        )

    barrier = pltpu.get_barrier_semaphore()
    chips = [(zz, yy) for zz in range(outer) for yy in range(inner)]

    @pl.when(c == 0)
    def _():
        signal(barrier, core_peer)

    for zz, yy in reversed(chips):
        @pl.when((zz >= z) & (yy >= y) & ((zz > z) | (yy > y)))
        def _():
            for cc in range(cores):
                signal(barrier, device(zz, yy, cc))

    chol_copy = pltpu.make_async_copy(chol_hbm, chol, chol_sem)
    order_copy = pltpu.make_async_copy(order_hbm, order_ref, order_sem)
    mean_copy = pltpu.make_async_copy(mean_hbm, mean_ref, mean_sem)
    noise_copy = pltpu.make_async_copy(noise_hbm, noise_ref, noise_sem)

    def span_of(owner, p):
        size = rows[p].shape[2]
        return pl.ds(pl.multiple_of(owner * pairs + starts[p], 128), size)

    own = [
        pltpu.make_async_copy(greens_hbm.at[:, span_of(me, p)], rows[p].at[me], own_sem.at[p])
        for p in range(2)
    ]
    a2a = []
    for p in range(2):
        a2a.append([])
        for k, offset in enumerate(offsets):
            target = shifted(*offset)
            a2a[p].append(remote(
                greens_hbm.at[:, span_of(target, p)], rows[p].at[me],
                a2a_send.at[p, k], a2a_recv.at[p, k], target,
            ))

    for copy in [order_copy, mean_copy, chol_copy, *own, noise_copy]:
        copy.start()
    below_here = cores * ((z + 1) * (y + 1) - 1) + c

    @pl.when(below_here > 0)
    def _():
        pl.semaphore_wait(barrier, below_here)

    here = z * inner + y

    @pl.when(c == cores - 1)
    def _():
        signal(near_sem.at[here], core_peer)
        for zz, yy in chips:
            @pl.when((zz <= z) & (yy <= y) & ((zz < z) | (yy < y)))
            def _():
                for cc in range(cores):
                    signal(near_sem.at[here], device(zz, yy, cc))

    for zv, yv in chips:
        far = 1 if zv < outer // 2 else -1
        above = [(zz, yy) for zz, yy in chips if zz >= zv and yy >= yv and (zz, yy) != (zv, yv)]
        below = {(zz, yy) for zz, yy in chips if zz <= zv and yy <= yv}
        waits, todo, left_over = [None, (zv, yv), *sorted(above, key=lambda a: (sum(a), a))], [], []
        known = below - {(zv, yv)}
        stage_of = {chip: 0 for chip in known}
        for stage, chip in enumerate(waits):
            if chip is not None:
                for zz, yy in chips:
                    if zz <= chip[0] and yy <= chip[1]:
                        stage_of.setdefault((zz, yy), stage)
        for p in range(2):
            for k, (dz, dy, dc) in enumerate(offsets):
                target = (zv + dz) % outer, (yv + dy) % inner
                r = (target[0] - zv) * far
                stage, *key = order_key((zv, yv), target, stage_of[target], r, dy, dc, p)
                todo.append((stage, key, p, k))
        todo.sort()

        @pl.when((z == zv) & (y == yv))
        def _():
            for stage, chip in enumerate(waits):
                if chip == (zv, yv):
                    @pl.when(c == 0)
                    def _():
                        pl.semaphore_wait(near_sem.at[zv * inner + yv], 1)
                elif chip is not None:
                    pl.semaphore_wait(near_sem.at[chip[0] * inner + chip[1]], 1)
                for when, _, p, k in todo:
                    if when == stage or (when > stage and stage == len(waits) - 1):
                        a2a[p][k].start()

    order_copy.wait()
    source = lax.broadcasted_iota(jnp.int32, (n * walkers, n * walkers), 0)
    chosen[...] = jnp.where(source == order_ref[...], 1.0, 0.0).T.astype(jnp.bfloat16)

    mean_copy.wait()
    chol_copy.wait()
    mean_rows = jnp.broadcast_to(mean_ref[...].astype(jnp.float32).reshape(1, pairs), (16, pairs)).astype(jnp.bfloat16)
    for q in range(CHUNKS):
        span = pl.ds(q * width, width)
        mean_mine[0, :, span] = contract(mean_rows, chol[span, :])[0:1, :]

    def mean_hop(at, stage, target):
        return remote(
            mean_mine.at[at], mean_in.at[stage], mean_send.at[stage], mean_recv.at[stage], target
        )

    core_hop = mean_hop(0, 0, core_peer)
    y_hop = mean_hop(1, 1, y_peer)
    z_hops = [mean_hop(2, 1 + dz, shifted(dz, 0, 0)) for dz in range(1, outer)]
    core_hop.start()
    core_hop.wait()
    mean_mine[1] = mean_mine[0] + mean_in[0]
    y_hop.start()

    def pick(p):
        own[p].wait()
        for copy in a2a[p]:
            copy.wait_recv()
        size = rows[p].shape[2]
        return jnp.dot(
            chosen[...], rows[p][...].reshape(n * walkers, size), preferred_element_type=jnp.float32
        ).astype(jnp.bfloat16)

    def add(p, picked, q):
        size = rows[p].shape[2]
        bias = contract(picked, chol[pl.ds(q * width, width), pl.ds(starts[p], size)])
        bias = bias.reshape(outer, inner, cores, walkers, width)
        for cc in range(cores):
            part[q, cc] = bias[:, :, cc] if p == 0 else part[q, cc] + bias[:, :, cc]

    picked = pick(0)
    for q in range(CHUNKS):
        add(0, picked, q)
    y_hop.wait()
    mean_mine[2] = mean_mine[1] + mean_in[1]
    for hop in z_hops:
        hop.start()
    picked = pick(1)

    half = outer // 2

    def core_copy(q, h):
        chips_of = pl.ds(h * half, half)
        return remote(
            part.at[q, 1 - c, chips_of], core_in.at[q, chips_of],
            core_send.at[q, h], core_recv.at[q, h], core_peer,
        )

    def y_copies(q, h):
        return (
            remote(y_code.at[q, h], y_in.at[q, h], y_send.at[q, h, 0], y_recv.at[q, h, 0], y_peer),
            remote(y_top.at[q, h], y_top_in.at[q, h], y_send.at[q, h, 1], y_recv.at[q, h, 1], y_peer),
        )

    def z_copies(q, h, at, slot, zz, target):
        return (
            remote(z_code.at[q, h, at], z_in.at[q, slot], z_send.at[q, zz, 0], z_recv.at[q, slot, 0], target),
            remote(z_top.at[q, h], z_top_in.at[q, slot], z_send.at[q, zz, 1], z_recv.at[q, slot, 1], target),
        )

    def both_cores(q, h, yy):
        z_part = pl.ds(half * h, half)
        return part[q, c, z_part, yy] + core_in[q, z_part, yy]

    def send_y(q, h):
        y_code[q, h], y_top[q, h] = encode(both_cores(q, h, 1 - y))
        for copy in y_copies(q, h):
            copy.start()

    def sum_cores(q):
        sum_half(q, 0)

    def sum_half(q, h):
        core_copy(q, h).wait()
        send_y(q, h)

    def sum_inner(q, h):
        for copy in y_copies(q, h):
            copy.wait()
        total = both_cores(q, h, y) + decode(y_in[q, h], y_top_in[q, h])
        z_out[q, half * h:half * (h + 1)] = total
        z_code[q, h], z_top[q, h] = encode(total)
        for at in range(half):
            zz = half * h + at

            @pl.when(z != zz)
            def _():
                for copy in z_copies(q, h, at, z, zz, device(zz, y, c)):
                    copy.start()

    def finish(q):
        span = pl.ds(q * width, width)
        raw = z_out[q, z]
        for dz in range(1, outer):
            zz = (z + dz) % outer
            for copy in z_copies(q, 0, 0, zz, zz, device(zz, y, c)):
                copy.wait_recv()
            raw = raw + decode(z_in[q, zz], z_top_in[q, zz])
        out_ref[:, span] = noise_ref[:, span] - (jnp.tanh(raw) - mean_mine[3, :, span])

    for step in range(CHUNKS + 2):
        if step < CHUNKS:
            add(1, picked, step)
            core_copy(step, 0).start()
        if step >= 2:
            sum_cores(step - 2)
        if step == CHUNKS - 1:
            for q in range(CHUNKS):
                core_copy(q, 1).start()
    for q in range(CHUNKS):
        sum_half(q, 1)
    for h in range(2):
        for q in range(CHUNKS):
            sum_inner(q, h)
    noise_copy.wait()
    for hop in z_hops:
        hop.wait()
    mean = mean_mine[2]
    for dz in range(1, outer):
        mean = mean + mean_in[1 + dz]
    mean_mine[3] = mean
    for q in range(CHUNKS):
        finish(q)
    for q in range(CHUNKS):
        for dz in range(1, outer):
            zz = (z + dz) % outer
            for copy in z_copies(q, 0, 0, zz, zz, device(zz, y, c)):
                copy.wait_send()
    for p in range(2):
        for copy in a2a[p]:
            copy.wait_send()


def fused_per_device(outer, inner, chol_vectors, mean_greens, greens, walker_order, noise_field):
    nchol, pairs = chol_vectors.shape
    walkers = greens.shape[0]
    n = outer * inner * 2
    width = nchol // CHUNKS
    last = pairs // LAST
    halves = (CHUNKS, 2, outer // 2, walkers, width)
    vmem = pl.BlockSpec(memory_space=pltpu.VMEM)
    hbm = pl.BlockSpec(memory_space=pltpu.HBM)
    dma = pltpu.SemaphoreType.DMA
    f32, i16 = jnp.float32, jnp.int16
    return pl.pallas_call(
        functools.partial(kernel, outer, inner),
        out_shape=pltpu.VMEM(noise_field.shape, f32),
        in_specs=[hbm] * 5,
        out_specs=vmem,
        scratch_shapes=[
            pltpu.VMEM((1, n * walkers), jnp.int32),
            pltpu.VMEM((pairs,), jnp.bfloat16),
            pltpu.VMEM(noise_field.shape, f32),
            pltpu.VMEM((nchol, pairs), jnp.bfloat16),
            pltpu.VMEM((n, walkers, pairs - last), jnp.bfloat16),
            pltpu.VMEM((n, walkers, last), jnp.bfloat16),
            pltpu.VMEM((n * walkers, n * walkers), jnp.bfloat16),
            pltpu.VMEM((CHUNKS, 2, outer, inner, walkers, width), f32),
            pltpu.VMEM((CHUNKS, outer, inner, walkers, width), f32),
            *[pltpu.VMEM(halves, i16), pltpu.VMEM((CHUNKS, 2, 1, width), f32)] * 2,
            pltpu.VMEM((CHUNKS, outer, walkers, width), f32),
            pltpu.VMEM(halves, i16), pltpu.VMEM((CHUNKS, 2, 1, width), f32),
            pltpu.VMEM((CHUNKS, outer, walkers, width), i16), pltpu.VMEM((CHUNKS, outer, 1, width), f32),
            pltpu.VMEM((4, 1, nchol), f32),
            pltpu.VMEM((1 + outer, 1, nchol), f32),
            dma, dma, dma, dma, dma((2,)), pltpu.SemaphoreType.REGULAR((outer * inner,)),
            dma((2, n - 1)), dma((2, n - 1)),
            dma((CHUNKS, 2)), dma((CHUNKS, 2)), dma((CHUNKS, 2, 2)), dma((CHUNKS, 2, 2)),
            dma((CHUNKS, outer, 2)), dma((CHUNKS, outer, 2)),
            dma((1 + outer,)), dma((1 + outer,)),
        ],
        compiler_params=pltpu.CompilerParams(
            collective_id=0, has_side_effects=True, vmem_limit_bytes=60 * 1024 * 1024
        ),
    )(walker_order[None, :], mean_greens, noise_field, chol_vectors, greens)


def solution(mesh):
    placed = (
        P(None, "chol"),
        P("chol"),
        P(("grp", "chol"), None),
        P("grp"),
        P(("grp", "chol"), None),
    )
    chips = mesh.shape["chol"] // 2
    inner = 1
    while (2 * inner) ** 2 <= chips:
        inner *= 2
    outer = chips // inner
    body = functools.partial(fused_per_device, outer, inner) if (outer, inner) == (4, 2) else plain_per_device
    return jax.shard_map(
        body, mesh=mesh, in_specs=placed, out_specs=P(("grp", "chol"), None), check_vma=False
    )
```
